256 devices in a mesh: tm: 64 (over x, y_hi, z), chan: 4 (over y_lo, core).
Axes of the slice: x: 4, y: 4 (y_hi: 2, y_lo: 2; y = y_hi * 2 + y_lo), z: 8, core: 2. Of those that a mesh axis runs over, the one named last changes fastest.
Arguments:
- features: bfloat16 [131072, 1024], P('tm', 'chan'), may hold values from -18 to 18
- rec_start: int32 [131072], P('tm'), may hold values from 0 to 131071, as said below
- rec_end: int32 [131072], P('tm'), may hold values from 1 to 131072, as said below
- w_value: bfloat16 [1024, 1024], P(None, 'chan'), may hold values from -0.1875 to 0.1875
- w_gate: bfloat16 [1024, 1024], P(None, 'chan'), may hold values from -0.1875 to 0.1875
- depth_kernel: bfloat16 [9, 1024], P(None, 'chan'), may hold values from -2 to 2
- norm_gain: bfloat16 [1024], P('chan'), may hold values from 0.099609375 to 1.8984375
- norm_shift: bfloat16 [1024], P('chan'), may hold values from -3 to 3
- w_down: bfloat16 [1024, 1024], P('chan'), may hold values from -0.1875 to 0.1875
Outputs:
- mixed: bfloat16 [131072, 1024], P('tm', 'chan')
The draws below stay inside these ranges and needn't reach their ends.
Inputs may be any that keep to these rules, and one draw needn't show every extreme that they name: Frames are packed recordings in order: rec_start[t] <= t < rec_end[t], all frames of a recording share both values, and a recording ends where the next starts. Frame 0 is a recording of its own, and so is the last frame. `rec_end`: as for rec_start.
All inputs are finite; a program needn't handle non-finite values.
Results may differ from the reference program's by a relative error of at most 0.012.
Values may be sent and summed in bfloat16 or wider, within the bound.
No kernel may reach another device: no remote copies, remote signals or barrier semaphores. Data moves between devices by JAX's collectives and lax.ppermute only.
A program may use at most 64 MiB of HBM per device.

```python
import jax
import jax.numpy as jnp
from jax import lax

D = 1024
C = 1024
KERNEL = 9
FRAMES = 131072


def segment_law(key):
    base = jax.random.fold_in(key, 11)
    first, second, third = jax.random.split(base, 3)
    index = jnp.arange(FRAMES, dtype=jnp.int32)
    fine_count = (FRAMES + 511) // 512
    coarse_count = (FRAMES + 16383) // 16384
    loud_count = (FRAMES + 4095) // 4096
    fine = jnp.clip(jax.random.normal(first, (fine_count, D), jnp.float32), -3.0, 3.0) * 0.6
    coarse = jnp.clip(jax.random.normal(second, (coarse_count, D), jnp.float32), -3.0, 3.0) * 0.6
    loud = jnp.exp(jax.random.uniform(third, (loud_count,), jnp.float32, -0.3567, 0.3365))
    offset = jnp.take(fine, index // 512, axis=0) + jnp.take(coarse, index // 16384, axis=0)
    loudness = jnp.take(loud, index // 4096, axis=0)
    return (offset, loudness[:, None])


def draw_features(key, part):
    frames = jnp.arange(FRAMES, dtype=jnp.float32)
    ramp = 1.0 + 2.0 * frames / max(FRAMES - 1, 1)
    offset, loudness = segment_law(key)
    noise = jnp.clip(jax.random.normal(key, (FRAMES, D), jnp.float32), -6.0, 6.0)
    values = (noise + offset) * loudness * (0.8 * ramp[:, None])
    return jnp.clip(values, -18.0, 18.0).astype(jnp.bfloat16)


def recording_bounds(key):
    base = jax.random.fold_in(key, 7)
    index = jnp.arange(FRAMES, dtype=jnp.int32)
    marks = jax.random.randint(base, (FRAMES,), 0, 48) == 0
    marks = marks | (index <= 1) | (index == FRAMES - 1)
    starts = lax.cummax(jnp.where(marks, index, 0), axis=0)
    following = jnp.roll(marks, -1) & (index < FRAMES - 1)
    upcoming = jnp.where(following, index + 1, FRAMES)
    ends = lax.cummin(upcoming, axis=0, reverse=True)
    return (starts.astype(jnp.int32), ends.astype(jnp.int32))


def draw_rec_start(key, part):
    return recording_bounds(key)[0]


def draw_rec_end(key, part):
    return recording_bounds(key)[1]


def steps_of(rng, shape, cuts, low, top_value):
    def one(dim, parts):
        heights = jax.random.uniform(jax.random.fold_in(jax.random.fold_in(rng, 6), dim), (parts,), jnp.float32, low / len(cuts), top_value / len(cuts))
        return jnp.repeat(jnp.exp(heights), shape[dim] // parts).reshape((-1,) + (1,) * (len(shape) - dim - 1))

    level = one(*cuts[0])
    for cut in cuts[1:]:
        level = level * one(*cut)
    return level


def normal_values(stream_key, extent, width, reach, cuts=(), kind=jnp.bfloat16):
    entries = width * jax.random.normal(stream_key, extent, jnp.float32)
    if cuts:
        entries = entries * steps_of(stream_key, extent, cuts, -0.22, 0.18)
    return jnp.clip(entries, -reach, reach).astype(kind)


def setup_inputs(seed: int = 0) -> dict:
    key_of = jax.random.split(jax.random.key(seed), 10)
    features = draw_features(jax.random.fold_in(key_of[9], 71), 0)
    rec_start = draw_rec_start(jax.random.fold_in(key_of[9], 71), 0)
    rec_end = draw_rec_end(jax.random.fold_in(key_of[9], 71), 0)
    w_value = normal_values(key_of[3], (D, C), D ** -0.5, 0.1875, ((1, 4),))
    w_gate = normal_values(key_of[4], (D, C), D ** -0.5, 0.1875, ((1, 4),))
    depth_kernel = normal_values(key_of[5], (KERNEL, C), KERNEL ** -0.5, 2.0, ((1, 4),))
    norm_gain = jnp.clip(1.0 + 0.18 * jax.random.normal(key_of[6], (C,), jnp.float32), 0.099609375, 1.8984375).astype(jnp.bfloat16)
    norm_shift = normal_values(key_of[7], (C,), 0.5, 3.0, ((0, 4),))
    w_down = normal_values(key_of[8], (C, D), C ** -0.5, 0.1875, ((0, 4),))
    return dict(features=features, rec_start=rec_start, rec_end=rec_end, w_value=w_value, w_gate=w_gate, depth_kernel=depth_kernel, norm_gain=norm_gain, norm_shift=norm_shift, w_down=w_down)


def reference(features, rec_start, rec_end, w_value, w_gate, depth_kernel, norm_gain, norm_shift, w_down):
    value = jnp.dot(features, w_value, preferred_element_type=jnp.float32)
    gate = jnp.dot(features, w_gate, preferred_element_type=jnp.float32)
    glu = (value * jax.nn.sigmoid(gate)).astype(jnp.bfloat16)
    half = KERNEL // 2
    padded = jnp.pad(glu, ((half, half), (0, 0)))
    frames = jnp.arange(FRAMES, dtype=jnp.int32)
    conv = jnp.zeros((FRAMES, C), jnp.float32)
    for tap in range(KERNEL):
        source = frames + (tap - half)
        usable = (source >= rec_start) & (source < rec_end)
        term = padded[tap:tap + FRAMES].astype(jnp.float32) * depth_kernel[tap].astype(jnp.float32)
        conv = conv + jnp.where(usable[:, None], term, jnp.float32(0.0))
    mean = lax.optimization_barrier(jnp.sum(conv, axis=0)) / FRAMES
    centred = conv - mean
    var = lax.optimization_barrier(jnp.sum(centred * centred, axis=0)) / FRAMES
    normed = centred / jnp.sqrt(var + 1e-05) * norm_gain.astype(jnp.float32) + norm_shift.astype(jnp.float32)
    swished = (normed * jax.nn.sigmoid(normed)).astype(jnp.bfloat16)
    return jnp.dot(swished, w_down, preferred_element_type=jnp.float32).astype(jnp.bfloat16)
```

```python
import functools

import jax
import jax.numpy as jnp
from jax import lax
from jax.experimental import pallas as pl
from jax.experimental.pallas import tpu as pltpu
from jax.sharding import PartitionSpec as P

AXES = ("tm", "chan")
F32, BF16 = jnp.float32, jnp.bfloat16
LANES = 128
TAIL = 32


def permute(value, move):
    tms, chans = lax.axis_size("tm"), lax.axis_size("chan")
    pairs = []
    for t in range(tms):
        for c in range(chans):
            to_t, to_c = move(t, c)
            pairs.append((t * chans + c, (to_t % tms) * chans + to_c))
    return lax.ppermute(value, AXES, pairs)


def over_link(t, c):
    return t, c ^ 2


def over_other_link(t, c):
    return (t ^ 8, c ^ 2)


def to_core(t, c):
    return t, c ^ 1


def to_diagonal(t, c):
    return t, c ^ 3


def stage_kernel(stage, taps_count, *refs):
    refs = list(refs)
    order = refs.pop(0)
    xs = [refs.pop(0) for _ in range(4)]
    wv, wg, taps, low, high = [refs.pop(0) for _ in range(5)]
    tail = refs.pop(0) if stage > 0 else None
    head = refs.pop(0) if stage == 3 else None
    conv_out, stats_out = refs.pop(0), refs.pop(0)
    tail_out = refs.pop(0) if stage < 3 else None
    head_out = refs.pop(0) if stage == 0 else None
    glu, conv = refs

    fresh, width = xs[0].shape[0], wv.shape[1]
    blocks = width // LANES
    half = taps_count // 2

    def put(row, value):
        for j in range(blocks):
            glu[j, row : row + value.shape[0], :] = value[:, j * LANES : (j + 1) * LANES].astype(F32)

    if tail is not None:
        put(0, tail[...])
    if head is not None:
        put(TAIL + fresh, head[...])

    depth = xs[0].shape[1]
    weights = []
    for w in (wv, wg):
        parts = [w[pl.ds(pl.multiple_of(order[i] * depth, depth), depth), :] for i in range(4)]
        weights.append(jnp.concatenate(parts, axis=0))
    row = 0
    while row < fresh:
        rows = min(256, fresh - row)
        if fresh - row - rows < 64:
            rows = fresh - row
        x = jnp.concatenate([ref[row : row + rows, :] for ref in xs], axis=1)
        value = jnp.dot(x, weights[0], preferred_element_type=F32)
        gate = jnp.dot(x, weights[1], preferred_element_type=F32)
        gated = (value * (0.5 + 0.5 * jnp.tanh(0.5 * gate))).astype(BF16)
        put(TAIL + row, gated)
        if head_out is not None and row == 0:
            head_out[...] = gated[:TAIL]
        if tail_out is not None and row + rows == fresh:
            tail_out[...] = gated[rows - TAIL :]
        row += rows

    total_rows = conv_out.shape[0]
    first = TAIL + 16 if stage == 0 else 16
    step = 32
    scale = [[jnp.broadcast_to(taps[k : k + 1, j * LANES : (j + 1) * LANES], (8, LANES)) for k in range(taps_count)] for j in range(blocks)]

    def conv_rows(source, target, rows, sums):
        lo, hi = low[pl.ds(target, rows), :], high[pl.ds(target, rows), :]
        out = []
        for j in range(blocks):
            acc = None
            for k in range(taps_count):
                shift = k - half
                term = glu[j, pl.ds(source + shift, rows), :]
                term = (term.reshape(rows // 8, 8, LANES) * scale[j][k][None]).reshape(rows, LANES)
                if shift < 0:
                    term = jnp.where(lo <= shift, term, 0.0)
                if shift > 0:
                    term = jnp.where(hi > shift, term, 0.0)
                acc = term if acc is None else acc + term
            conv[j, pl.ds(target, rows), :] = acc
            out.append(sums[j] + jnp.sum(acc.reshape(rows // 8, 8, LANES), axis=0))
        return tuple(out)

    zero = tuple(jnp.zeros((8, LANES), F32) for _ in range(blocks))
    straight = total_rows - 16 if stage == 3 else total_rows

    def body(i, sums):
        target = pl.multiple_of(i * step, step)
        return conv_rows(target + first, target, step, sums)

    whole = straight // step
    sums = lax.fori_loop(0, whole, body, zero)
    if straight % step:
        sums = conv_rows(first + whole * step, whole * step, straight % step, sums)
    if stage == 3:
        sums = conv_rows(TAIL + fresh, straight, 16, sums)

    means = [jnp.sum(s, axis=0, keepdims=True) * (1.0 / total_rows) for s in sums]
    means8 = [jnp.broadcast_to(m, (8, LANES)) for m in means]

    def centre(i, squares):
        target = pl.multiple_of(i * step, step)
        out = []
        for j in range(blocks):
            c = conv[j, pl.ds(target, step), :].reshape(step // 8, 8, LANES) - means8[j][None]
            conv_out[pl.ds(target, step), j * LANES : (j + 1) * LANES] = c.reshape(step, LANES).astype(BF16)
            out.append(squares[j] + jnp.sum(c * c, axis=0))
        return tuple(out)

    squares = lax.fori_loop(0, total_rows // step, centre, zero)
    for j in range(blocks):
        stats_out[0:1, j * LANES : (j + 1) * LANES] = means[j]
        stats_out[1:2, j * LANES : (j + 1) * LANES] = jnp.sum(squares[j], axis=0, keepdims=True)


def stage_call(stage, order, xs, wv, wg, taps, taps_count, low, high, tail=None, head=None):
    fresh, width = xs[0].shape[0], wv.shape[1]
    rows = low.shape[0]
    outs = [jax.ShapeDtypeStruct((rows, width), BF16), jax.ShapeDtypeStruct((8, width), F32)]
    edge = jax.ShapeDtypeStruct((TAIL, width), BF16)
    if stage < 3:
        outs.append(edge)
    if stage == 0:
        outs.append(edge)
    operands = [order, *xs, wv, wg, taps, low, high]
    if stage > 0:
        operands.append(tail)
    if stage == 3:
        operands.append(head)
    vmem = pl.BlockSpec(memory_space=pltpu.VMEM)
    return pl.pallas_call(
        functools.partial(stage_kernel, stage, taps_count),
        out_shape=outs,
        in_specs=[pl.BlockSpec(memory_space=pltpu.SMEM)] + [vmem] * (len(operands) - 1),
        out_specs=[vmem] * len(outs),
        scratch_shapes=[
            pltpu.VMEM((width // LANES, TAIL + fresh + TAIL + 16, LANES), F32),
            pltpu.VMEM((width // LANES, rows, LANES), F32),
        ],
        cost_estimate=pl.CostEstimate(
            flops=4 * fresh * 4 * xs[0].shape[1] * width, transcendentals=fresh * width, bytes_accessed=4 << 20
        ),
        name=f"stage{stage}",
    )(*operands)


def finish_kernel(pieces, bounds, *refs):
    convs = refs[: 4 * pieces]
    scales, means, weights, out = refs[4 * pieces : 4 * pieces + 4]
    for piece in range(pieces):
        rows = convs[piece].shape[0]
        parts = []
        for block in range(4):
            width = convs[block * pieces + piece].shape[1]
            a = scales[block, 0:1, :] * 0.5
            b = scales[block, 1:2, :] * 0.5 + means[block, piece : piece + 1, :] * a
            h = convs[block * pieces + piece][...].astype(F32) * a + b
            parts.append((h + h * jnp.tanh(h)).astype(BF16))
        swished = jnp.concatenate(parts, axis=1)
        result = jnp.dot(swished, weights[...], preferred_element_type=F32).astype(BF16)
        at = 0
        for start, size in bounds[piece]:
            out[start : start + size, :] = result[at : at + size]
            at += size


def body(
    features, rec_start, rec_end, w_value, w_gate, depth_kernel, norm_gain, norm_shift, w_down
):
    rows, width = features.shape
    taps_count = depth_kernel.shape[0]
    tms = lax.axis_size("tm")
    total = rows * tms
    me, chan = lax.axis_index("tm"), lax.axis_index("chan")
    chunk = rows // 4

    after = permute(features[:8], lambda t, c: (t - 1, c))
    before = permute(features[rows - 8 :], lambda t, c: (t + 1, c))

    chunks = [features[k * chunk : (k + 1) * chunk] for k in range(4)]
    chunks[3] = jnp.concatenate([chunks[3], after, before], axis=0)
    linked = [permute(piece, over_link) for piece in chunks]
    mates = [permute(piece, to_core) for piece in chunks]
    far = [permute(piece, to_core) for piece in linked]
    order = jnp.stack([chan, chan ^ 1, chan ^ 2, chan ^ 3]).astype(jnp.int32)

    wv_other = permute(w_value, over_other_link)
    wg_other = permute(w_gate, over_other_link)
    taps = jnp.pad(depth_kernel.astype(F32), ((0, 16 - taps_count), (0, 0)))
    taps_other = permute(taps, over_other_link)

    chip = chan // 2
    down_sent = lax.dynamic_slice(w_down, (0, (1 - chip) * 2 * width), (width, 2 * width))
    down_other = permute(down_sent, over_other_link)
    mine, mates_part = chan % 2, 1 - chan % 2
    down_own = lax.dynamic_slice(w_down, (0, chip * 2 * width), (width, 2 * width))
    pair = jnp.concatenate([down_own, down_other], axis=0)
    down_mate = permute(lax.dynamic_slice(pair, (0, mates_part * width), (2 * width, width)), to_core)
    down = jnp.concatenate([lax.dynamic_slice(pair, (0, mine * width), (2 * width, width)), down_mate], axis=0)

    frames = me * rows + jnp.arange(rows, dtype=jnp.int32)
    lows, highs = rec_start - frames, rec_end - frames
    edges = [16, chunk - 16, 2 * chunk - 16, 3 * chunk - 16, rows]

    def spread(vector, k):
        part = vector[edges[k] : edges[k + 1]]
        if k == 3:
            part = jnp.concatenate([part, vector[:16]])
        return jnp.broadcast_to(part[:, None], (part.shape[0], LANES))

    low, high = [spread(lows, k) for k in range(4)], [spread(highs, k) for k in range(4)]

    def block_of(wv, wg, taps):
        convs, stats, tail, head = [], [], None, None
        for k in range(4):
            xs = [chunks[k], mates[k], linked[k], far[k]]
            out = stage_call(k, order, xs, wv, wg, taps, taps_count, low[k], high[k], tail, head)
            convs.append(out[0])
            stats.append(out[1])
            tail = out[2] if k < 3 else None
            head = out[3] if k == 0 else head
        return convs, stats

    own_conv, own_stats = block_of(w_value, w_gate, taps)
    other_conv, other_stats = block_of(wv_other, wg_other, taps_other)

    own_means = jnp.stack([s[0] for s in own_stats])
    other_means = jnp.stack([s[0] for s in other_stats])
    mate_conv = [permute(c, to_core) for c in own_conv]
    mate_other_conv = [permute(c, to_core) for c in other_conv]
    pair_means = jnp.stack([own_means, other_means])
    means = jnp.concatenate([pair_means, permute(pair_means, to_core)], axis=0)

    counts = jnp.array([c.shape[0] for c in own_conv], F32)[:, None]
    squares = jnp.stack([s[1] for s in own_stats])
    mean_here = jnp.sum(own_means * counts, axis=0) / rows
    spread_here = jnp.sum(squares + counts * (own_means - mean_here) ** 2, axis=0)
    sent = jnp.stack([mean_here, spread_here])
    got = lax.all_to_all(jnp.broadcast_to(sent[None], (tms, 2, width)), "tm", 0, 0)
    mean = jnp.sum(got[:, 0], axis=0) / tms
    var = jnp.sum(got[:, 1] + rows * (got[:, 0] - mean) ** 2, axis=0) / total
    scale = norm_gain.astype(F32) / jnp.sqrt(var + 1e-05)
    own_scale = jnp.stack([scale, norm_shift.astype(F32) - mean * scale])
    scales = jnp.stack(
        [own_scale, permute(own_scale, over_link), permute(own_scale, to_core), permute(own_scale, to_diagonal)]
    )

    bounds = [[(edges[k], edges[k + 1] - edges[k])] for k in range(4)]
    bounds[3].append((0, 16))
    vmem = pl.BlockSpec(memory_space=pltpu.VMEM)
    return pl.pallas_call(
        functools.partial(finish_kernel, 4, bounds),
        out_shape=jax.ShapeDtypeStruct((rows, width), BF16),
        in_specs=[vmem] * 19,
        out_specs=vmem,
        cost_estimate=pl.CostEstimate(flops=2 * rows * 4 * width * width, transcendentals=rows * 4 * width, bytes_accessed=6 << 20),
        name="finish",
    )(*own_conv, *other_conv, *mate_conv, *mate_other_conv, scales, means, down)


def solution(mesh):
    in_specs = (
        P("tm", "chan"),
        P("tm"),
        P("tm"),
        P(None, "chan"),
        P(None, "chan"),
        P(None, "chan"),
        P("chan"),
        P("chan"),
        P("chan", None),
    )
    out_specs = P("tm", "chan")
    return jax.shard_map(body, mesh=mesh, in_specs=in_specs, out_specs=out_specs, check_vma=False)
```

```python
import functools

import jax
import jax.numpy as jnp
from jax import lax
from jax.experimental import pallas as pl
from jax.experimental.pallas import tpu as pltpu
from jax.sharding import PartitionSpec as P

AXES = ("tm", "chan")
F32, BF16 = jnp.float32, jnp.bfloat16
LANES = 128
TAIL = 32


def permute(value, move):
    tms, chans = lax.axis_size("tm"), lax.axis_size("chan")
    pairs = []
    for t in range(tms):
        for c in range(chans):
            to_t, to_c = move(t, c)
            pairs.append((t * chans + c, (to_t % tms) * chans + to_c))
    return lax.ppermute(value, AXES, pairs)


def over_link(t, c):
    return t, c ^ 2


def over_other_link(t, c):
    return t ^ 8, c ^ 2


def across(t, c):
    return t ^ 16, c


def to_core(t, c):
    return t, c ^ 1


def to_diagonal(t, c):
    return t, c ^ 3


def near(value):
    return pltpu.with_memory_space_constraint(value, pltpu.VMEM)


STEP = 16


def stage_kernel(stage, taps_count, frames, *refs):
    refs = list(refs)
    place = refs.pop(0)
    xs = [refs.pop(0) for _ in range(4)]
    halos = [refs.pop(0) for _ in range(4)] if stage == 3 else None
    wv, wg = refs.pop(0), refs.pop(0)
    fetched = [[refs.pop(0) for _ in range(2)] for _ in range(2)]
    taps, taps_other, low, high = [refs.pop(0) for _ in range(4)]
    tail = refs.pop(0) if stage > 0 else None
    head = refs.pop(0) if stage == 3 else None
    earlier = [refs.pop(0) for _ in range(3)] if stage == 3 else None
    conv_out, stats_out = refs.pop(0), refs.pop(0)
    tail_out = refs.pop(0) if stage < 3 else None
    head_out = refs.pop(0) if stage == 0 else None
    sent_out = refs.pop(0) if stage == 3 else None
    glu, conv = refs

    fresh, depth = xs[0].shape
    width = wv.shape[1]
    blocks = 2 * width // LANES
    half = taps_count // 2

    def put(row, value):
        for j in range(blocks):
            glu[j, row : row + value.shape[0], :] = value[:, j * LANES : (j + 1) * LANES].astype(F32)

    def columns(j):
        return slice(j * LANES, (j + 1) * LANES)

    starts = [pl.multiple_of(place[i] * depth, depth) for i in range(4)]

    def ordered(parts):
        return jnp.concatenate(
            [jnp.concatenate([w[pl.ds(s, depth), :] for w in parts], axis=1) for s in starts], axis=0
        )

    own_v, own_g = ordered([wv]), ordered([wg])
    first_w, second_w = ordered(fetched[0]), ordered(fetched[1])
    swap = place[4] == 1

    def gated_of(x):
        value = jnp.dot(x, own_v, preferred_element_type=F32)
        gate = jnp.dot(x, own_g, preferred_element_type=F32)
        one = jnp.dot(x, first_w, preferred_element_type=F32)
        two = jnp.dot(x, second_w, preferred_element_type=F32)
        value_other, gate_other = jnp.where(swap, two, one), jnp.where(swap, one, two)
        own = (value * (0.5 + 0.5 * jnp.tanh(0.5 * gate))).astype(BF16)
        other = (value_other * (0.5 + 0.5 * jnp.tanh(0.5 * gate_other))).astype(BF16)
        return jnp.concatenate([own, other], axis=1)

    if tail is not None:
        put(0, tail[...])
    for row in range(0, fresh, 256):
        gated = gated_of(jnp.concatenate([ref[row : row + 256, :] for ref in xs], axis=1))
        put(TAIL + row, gated)
        if head_out is not None and row == 0:
            head_out[...] = gated[:TAIL]
        if tail_out is not None and row + 256 == fresh:
            tail_out[...] = gated[256 - TAIL :]
    if stage == 3:
        put(TAIL + fresh, gated_of(jnp.concatenate([ref[...] for ref in halos], axis=1)))
        put(TAIL + fresh + 16, head[...])

    total_rows = conv_out.shape[0]
    first = TAIL + 16 if stage == 0 else 16
    scale = [
        [
            jnp.broadcast_to((taps if j < blocks // 2 else taps_other)[k : k + 1, columns(j % (blocks // 2))], (8, LANES))
            for k in range(taps_count)
        ]
        for j in range(blocks)
    ]

    def conv_rows(source, target, sums):
        lo, hi = low[pl.ds(target, STEP), :], high[pl.ds(target, STEP), :]
        out = []
        for j in range(blocks):
            acc = None
            for k in range(taps_count):
                shift = k - half
                term = glu[j, pl.ds(source + shift, STEP), :]
                term = (term.reshape(STEP // 8, 8, LANES) * scale[j][k][None]).reshape(STEP, LANES)
                if shift < 0:
                    term = jnp.where(lo <= shift, term, 0.0)
                if shift > 0:
                    term = jnp.where(hi > shift, term, 0.0)
                acc = term if acc is None else acc + term
            conv[j, pl.ds(target, STEP), :] = acc
            out.append(sums[j] + jnp.sum(acc.reshape(STEP // 8, 8, LANES), axis=0))
        return tuple(out)

    zero = tuple(jnp.zeros((8, LANES), F32) for _ in range(blocks))
    straight = total_rows - 16 if stage == 3 else total_rows

    def step(i, sums):
        target = pl.multiple_of(i * STEP, STEP)
        return conv_rows(target + first, target, sums)

    sums = lax.fori_loop(0, straight // STEP, step, zero, unroll=2)
    if stage == 3:
        sums = conv_rows(TAIL + fresh + 16, straight, sums)

    means = [jnp.sum(s, axis=0, keepdims=True) * (1.0 / total_rows) for s in sums]
    means8 = [jnp.broadcast_to(m, (8, LANES)) for m in means]

    def centre(i, squares):
        target = pl.multiple_of(i * STEP, STEP)
        out = []
        for j in range(blocks):
            c = conv[j, pl.ds(target, STEP), :].reshape(STEP // 8, 8, LANES) - means8[j][None]
            conv_out[pl.ds(target, STEP), columns(j)] = c.reshape(STEP, LANES).astype(BF16)
            out.append(squares[j] + jnp.sum(c * c, axis=0))
        return tuple(out)

    squares = lax.fori_loop(0, total_rows // STEP, centre, zero, unroll=2)
    squares = [jnp.sum(q, axis=0, keepdims=True) for q in squares]
    for j in range(blocks):
        stats_out[0:1, columns(j)] = means[j]
        stats_out[1:2, columns(j)] = squares[j]
        stats_out[2:3, columns(j)] = jnp.full((1, LANES), float(total_rows), F32)
    if stage == 3:
        for j in range(blocks // 2):
            parts = [(ref[2:3, columns(j)], ref[0:1, columns(j)], ref[1:2, columns(j)]) for ref in earlier]
            parts.append((jnp.full((1, LANES), float(total_rows), F32), means[j], squares[j]))
            mean = sum(n * m for n, m, _ in parts) * (1.0 / frames)
            spread = sum(q + n * (m - mean) * (m - mean) for n, m, q in parts)
            sent_out[j : j + 1, :] = mean
            sent_out[blocks // 2 + j : blocks // 2 + j + 1, :] = spread


def stage_call(stage, taps_count, frames, place, xs, halos, wv, wg, fetched, taps, taps_other, low, high, tail, head, earlier):
    fresh, width = xs[0].shape[0], wv.shape[1]
    rows = low.shape[0]
    edge = pltpu.VMEM((TAIL, 2 * width), BF16)
    outs = [pltpu.VMEM((rows, 2 * width), BF16), pltpu.VMEM((8, 2 * width), F32)]
    operands = list(xs)
    if stage == 3:
        operands += halos
    operands += [wv, wg, *fetched[0], *fetched[1], taps, taps_other, low, high]
    if stage > 0:
        operands.append(tail)
    if stage == 3:
        operands += [head, *earlier]
    if stage < 3:
        outs.append(edge)
    if stage == 0:
        outs.append(edge)
    if stage == 3:
        outs.append(pltpu.VMEM((2 * width // LANES, LANES), F32))
    vmem = pl.BlockSpec(memory_space=pltpu.VMEM)
    return pl.pallas_call(
        functools.partial(stage_kernel, stage, taps_count, frames),
        out_shape=outs,
        in_specs=[pl.BlockSpec(memory_space=pltpu.SMEM)] + [vmem] * len(operands),
        out_specs=[vmem] * len(outs),
        scratch_shapes=[
            pltpu.VMEM((2 * width // LANES, TAIL + fresh + 16 + TAIL, LANES), F32),
            pltpu.VMEM((2 * width // LANES, rows, LANES), F32),
        ],
        cost_estimate=pl.CostEstimate(
            flops=16 * fresh * xs[0].shape[1] * width, transcendentals=fresh * width, bytes_accessed=4 << 20
        ),
        compiler_params=pltpu.CompilerParams(vmem_limit_bytes=16 << 20),
        name=f"stage{stage}",
    )(place, *[near(o) for o in operands])


def finish_kernel(pieces, bounds, *refs):
    convs, mates = refs[:pieces], refs[pieces : 2 * pieces]
    stats, mate_stats = refs[2 * pieces : 3 * pieces], refs[3 * pieces : 4 * pieces]
    scales, weights, out = refs[4 * pieces :]
    width = out.shape[1]
    for piece in range(pieces):
        parts = []
        for block in range(4):
            cut = slice(block % 2 * width, (block % 2 + 1) * width)
            source = (convs if block < 2 else mates)[piece]
            mean = (stats if block < 2 else mate_stats)[piece][0:1, cut]
            a = scales[2 * block : 2 * block + 1, :] * 0.5
            b = scales[2 * block + 1 : 2 * block + 2, :] * 0.5 + mean * a
            h = source[:, cut].astype(F32) * a + b
            parts.append((h + h * jnp.tanh(h)).astype(BF16))
        result = jnp.dot(jnp.concatenate(parts, axis=1), weights[...], preferred_element_type=F32).astype(BF16)
        at = 0
        for start, size in bounds[piece]:
            out[start : start + size, :] = result[at : at + size]
            at += size


def body(
    features, rec_start, rec_end, w_value, w_gate, depth_kernel, norm_gain, norm_shift, w_down
):
    rows, width = features.shape
    taps_count = depth_kernel.shape[0]
    tms = lax.axis_size("tm")
    total = rows * tms
    me, chan = lax.axis_index("tm"), lax.axis_index("chan")
    chunk = rows // 4

    first_chunk = features[:chunk]
    rest, _ = lax.optimization_barrier((features, first_chunk))
    chunks = [first_chunk] + [rest[k * chunk : (k + 1) * chunk] for k in range(1, 4)]
    linked = [permute(piece, over_link) for piece in chunks]

    swap = me // 16 % 2
    fetched = [[], []]
    for h in range(width // LANES):
        cut = slice(h * LANES, (h + 1) * LANES)
        part = permute(jnp.where(swap == 0, w_value[:, cut], w_gate[:, cut]), over_other_link)
        fetched[0].append(part)
        fetched[1].append(permute(part, across))
    place = jnp.stack([chan, chan ^ 1, chan ^ 2, chan ^ 3, swap]).astype(jnp.int32)

    halo = jnp.concatenate(
        [
            permute(rest[:8], lambda t, c: (t - 1, c)),
            permute(rest[rows - 8 :], lambda t, c: (t + 1, c)),
        ],
        axis=0,
    )
    halo_linked = permute(halo, over_link)
    halos = [halo, permute(halo, to_core), halo_linked, permute(halo_linked, to_core)]

    mates = [permute(piece, to_core) for piece in chunks]
    far = [permute(piece, to_core) for piece in linked]

    taps = jnp.pad(depth_kernel.astype(F32), ((0, 16 - taps_count), (0, 0)))
    taps_other = permute(taps, over_other_link)

    chip = chan // 2
    down_sent = lax.dynamic_slice(w_down, (0, (1 - chip) * 2 * width), (width, 2 * width))
    down_other = permute(down_sent, over_other_link)
    mine, mates_part = chan % 2, 1 - chan % 2
    down_own = lax.dynamic_slice(w_down, (0, chip * 2 * width), (width, 2 * width))
    pair = jnp.concatenate([down_own, down_other], axis=0)
    down_mate = permute(lax.dynamic_slice(pair, (0, mates_part * width), (2 * width, width)), to_core)
    down = jnp.concatenate([lax.dynamic_slice(pair, (0, mine * width), (2 * width, width)), down_mate], axis=0)

    frames = me * rows + jnp.arange(rows, dtype=jnp.int32)
    lows, highs = rec_start - frames, rec_end - frames
    edges = [16, chunk - 16, 2 * chunk - 16, 3 * chunk - 16, rows]

    def spread(vector, k):
        part = vector[edges[k] : edges[k + 1]]
        if k == 3:
            part = jnp.concatenate([part, vector[:16]])
        return jnp.broadcast_to(part[:, None], (part.shape[0], LANES))

    convs, stats, tail, head = [], [], None, None
    for k in range(4):
        xs = [chunks[k], mates[k], linked[k], far[k]]
        out = stage_call(
            k, taps_count, rows, place, xs, halos, w_value, w_gate, fetched, taps, taps_other,
            spread(lows, k), spread(highs, k), tail, head, stats,
        )
        convs.append(out[0])
        stats.append(out[1])
        tail = out[2] if k < 3 else None
        head = out[3] if k == 0 else head
    sent = out[2]

    mate_convs = [permute(c, to_core) for c in convs]
    mate_stats = [permute(s, to_core) for s in stats]

    half = sent.shape[0] // 2
    got = lax.all_to_all(jnp.broadcast_to(sent[None], (tms,) + sent.shape), "tm", 0, 0)
    mean = jnp.sum(got[:, :half], axis=0) / tms
    var = jnp.sum(got[:, half:] + rows * (got[:, :half] - mean) ** 2, axis=0) / total
    scale = norm_gain.astype(F32).reshape(half, LANES) / jnp.sqrt(var + 1e-05)
    shift = norm_shift.astype(F32).reshape(half, LANES) - mean * scale
    own_scale = jnp.stack([scale.reshape(width), shift.reshape(width)])
    scales = jnp.concatenate(
        [own_scale, permute(own_scale, over_link), permute(own_scale, to_core), permute(own_scale, to_diagonal)]
    )

    bounds = [[(edges[k], edges[k + 1] - edges[k])] for k in range(4)]
    bounds[3].append((0, 16))
    vmem = pl.BlockSpec(memory_space=pltpu.VMEM)
    operands = [*convs, *mate_convs, *stats, *mate_stats, scales, down]
    return pl.pallas_call(
        functools.partial(finish_kernel, 4, bounds),
        out_shape=jax.ShapeDtypeStruct((rows, width), BF16),
        in_specs=[vmem] * len(operands),
        out_specs=vmem,
        cost_estimate=pl.CostEstimate(
            flops=8 * rows * width * width, transcendentals=rows * 4 * width, bytes_accessed=6 << 20
        ),
        compiler_params=pltpu.CompilerParams(vmem_limit_bytes=16 << 20),
        name="finish",
    )(*[near(o) for o in operands])


def solution(mesh):
    in_specs = (
        P("tm", "chan"),
        P("tm"),
        P("tm"),
        P(None, "chan"),
        P(None, "chan"),
        P(None, "chan"),
        P("chan"),
        P("chan"),
        P("chan", None),
    )
    out_specs = P("tm", "chan")
    return jax.shard_map(body, mesh=mesh, in_specs=in_specs, out_specs=out_specs, check_vma=False)
```

```python
import functools

import jax
import jax.numpy as jnp
from jax import lax
from jax.experimental import pallas as pl
from jax.experimental.pallas import tpu as pltpu
from jax.sharding import PartitionSpec as P


AXES = ("tm", "chan")
F32, BF16 = jnp.float32, jnp.bfloat16
LANES = 128
TAIL = 32


def permute(value, move):
    tms, chans = lax.axis_size("tm"), lax.axis_size("chan")
    pairs = []
    for t in range(tms):
        for c in range(chans):
            to_t, to_c = move(t, c)
            if 0 <= to_t < tms:
                pairs.append((t * chans + c, to_t * chans + to_c))
    return lax.ppermute(value, AXES, pairs)


def over_link(t, c):
    return t, c ^ 2


def over_other_link(t, c):
    return t ^ 8, c ^ 2


def to_core(t, c):
    return t, c ^ 1


def to_diagonal(t, c):
    return t, c ^ 3


def near(value):
    return pltpu.with_memory_space_constraint(value, pltpu.VMEM)


STEP = 16


def stage_kernel(stage, taps_count, rows, edge, *refs):
    refs = list(refs)
    own, mate, linked, far = [refs.pop(0) for _ in range(4)]
    halos = [refs.pop(0) for _ in range(4)] if stage == 3 else None
    weights = [refs.pop(0) for _ in range(2)]
    taps, start, end = [refs.pop(0) for _ in range(3)]
    tail = refs.pop(0) if stage > 0 else None
    head = refs.pop(0) if stage == 3 else None
    earlier = [refs.pop(0) for _ in range(3)] if stage == 3 else None
    conv_out, stats_out = refs.pop(0), refs.pop(0)
    tail_out = refs.pop(0) if stage < 3 else None
    head_out = refs.pop(0) if stage == 0 else None
    sent_out = refs.pop(0) if stage == 3 else None
    glu, conv = refs

    fresh = linked.shape[0]
    width = weights[0].shape[1]
    blocks = width // LANES
    half = taps_count // 2
    position = lax.axis_index("tm")

    def columns(j):
        return slice(j * LANES, (j + 1) * LANES)

    def put(row, value):
        for j in range(blocks):
            glu[j, row : row + value.shape[0], :] = value[:, columns(j)].astype(F32)

    def gated_of(parts):
        x = jnp.concatenate(parts, axis=1)
        value, gate = [jnp.dot(x, w[...], preferred_element_type=F32) for w in weights]
        return (value * (0.5 + 0.5 * jnp.tanh(0.5 * gate))).astype(BF16)

    if tail is not None:
        put(0, tail[...])
    for row in range(0, fresh, 256):
        at = stage * fresh + row
        parts = [own[at : at + 256, :], mate[at : at + 256, :], linked[row : row + 256, :], far[row : row + 256, :]]
        if halos is not None and row + 256 == fresh:
            parts = [jnp.concatenate([part, halo[...]], axis=0) for part, halo in zip(parts, halos)]
        gated = gated_of(parts)
        put(TAIL + row, gated)
        if head_out is not None and row == 0:
            head_out[...] = gated[:TAIL]
        if tail_out is not None and row + 256 == fresh:
            tail_out[...] = gated[256 - TAIL :]
    if stage == 3:
        put(TAIL + fresh + 16, head[...])

    total_rows = conv_out.shape[0]
    first = TAIL + 16 if stage == 0 else 16
    scale = [[jnp.broadcast_to(taps[k : k + 1, columns(j)], (8, LANES)) for k in range(taps_count)] for j in range(blocks)]
    line = lax.broadcasted_iota(jnp.int32, (STEP, LANES), 0) + position * rows

    def conv_rows(source, target, row, sums):
        frame = line + row
        lo, hi = start[pl.ds(target, STEP), :] - frame, end[pl.ds(target, STEP), :] - frame
        out = []
        for j in range(blocks):
            acc = None
            for k in range(taps_count):
                shift = k - half
                term = glu[j, pl.ds(source + shift, STEP), :]
                term = (term.reshape(STEP // 8, 8, LANES) * scale[j][k][None]).reshape(STEP, LANES)
                if shift < 0:
                    term = jnp.where(lo <= shift, term, 0.0)
                if shift > 0:
                    term = jnp.where(hi > shift, term, 0.0)
                acc = term if acc is None else acc + term
            conv[j, pl.ds(target, STEP), :] = acc
            out.append(sums[j] + jnp.sum(acc.reshape(STEP // 8, 8, LANES), axis=0))
        return tuple(out)

    zero = tuple(jnp.zeros((8, LANES), F32) for _ in range(blocks))
    straight = total_rows - 16 if stage == 3 else total_rows

    def step(i, sums):
        target = pl.multiple_of(i * STEP, STEP)
        return conv_rows(target + first, target, target + edge, sums)

    sums = lax.fori_loop(0, straight // STEP, step, zero, unroll=UNROLL)
    if stage == 3:
        sums = conv_rows(TAIL + fresh + 16, straight, 0, sums)

    means = [jnp.sum(s, axis=0, keepdims=True) * (1.0 / total_rows) for s in sums]
    means8 = [jnp.broadcast_to(m, (8, LANES)) for m in means]

    def centre(i, squares):
        target = pl.multiple_of(i * STEP, STEP)
        out = []
        for j in range(blocks):
            c = conv[j, pl.ds(target, STEP), :].reshape(STEP // 8, 8, LANES) - means8[j][None]
            conv_out[pl.ds(target, STEP), columns(j)] = c.reshape(STEP, LANES).astype(BF16)
            out.append(squares[j] + jnp.sum(c * c, axis=0))
        return tuple(out)

    squares = lax.fori_loop(0, total_rows // STEP, centre, zero, unroll=UNROLL)
    squares = [jnp.sum(q, axis=0, keepdims=True) for q in squares]
    count = jnp.full((1, LANES), float(total_rows), F32)
    if stage < 3:
        for j in range(blocks):
            stats_out[0:1, columns(j)] = means[j]
            stats_out[1:2, columns(j)] = squares[j]
            stats_out[2:3, columns(j)] = count
    else:
        for j in range(blocks):
            for k in range(3):
                stats_out[k : k + 1, columns(j)] = earlier[k][0:1, columns(j)]
            stats_out[3:4, columns(j)] = means[j]
    if sent_out is not None:
        totals = []
        for j in range(blocks):
            parts = [(ref[2:3, columns(j)], ref[0:1, columns(j)], ref[1:2, columns(j)]) for ref in earlier]
            parts.append((count, means[j], squares[j]))
            mean = sum(n * m for n, m, _ in parts) * (1.0 / rows)
            totals.append((mean, sum(q + n * (m - mean) * (m - mean) for n, m, q in parts)))
        piece = jnp.concatenate([t[0] for t in totals] + [t[1] for t in totals], axis=0)
        for i in range(sent_out.shape[0]):
            sent_out[i] = piece


UNROLL = 4


def stage_call(stage, taps_count, rows, edge, devices, xs, halos, weights, taps, start, end, tail, head, earlier):
    fresh, width = xs[2].shape[0], weights[0].shape[1]
    count = start.shape[0]
    margin = pltpu.VMEM((TAIL, width), BF16)
    outs = [pltpu.HBM((count, width), BF16), pltpu.VMEM((8, width), F32)]
    operands = list(xs)
    if stage == 3:
        operands += halos
    operands += [*weights, taps, start, end]
    if stage > 0:
        operands.append(tail)
    if stage == 3:
        operands += [head, *earlier]
    if stage < 3:
        outs.append(margin)
    if stage == 0:
        outs.append(margin)
    if stage == 3:
        outs.append(pltpu.VMEM((devices, 2 * width // LANES, LANES), F32))
    vmem = pl.BlockSpec(memory_space=pltpu.VMEM)
    return pl.pallas_call(
        functools.partial(stage_kernel, stage, taps_count, rows, edge),
        out_shape=outs,
        in_specs=[vmem] * len(operands),
        out_specs=[vmem] * len(outs),
        scratch_shapes=[
            pltpu.VMEM((width // LANES, TAIL + fresh + 16 + TAIL, LANES), F32),
            pltpu.VMEM((width // LANES, count, LANES), F32),
        ],
        cost_estimate=pl.CostEstimate(
            flops=16 * fresh * width * width, transcendentals=fresh * width, bytes_accessed=4 << 20
        ),
        compiler_params=pltpu.CompilerParams(vmem_limit_bytes=12 << 20),
    )(*[near(o) for o in operands])


def lay_out_kernel(value, gate, own_value, own_gate):
    depth = value.shape[0] // 4
    chan = lax.axis_index("chan")
    for i in range(4):
        rows = pl.ds(pl.multiple_of((chan ^ i) * depth, depth), depth)
        own_value[i * depth : (i + 1) * depth, :] = value[rows, :]
        own_gate[i * depth : (i + 1) * depth, :] = gate[rows, :]


def columns_kernel(down, *outs):
    width = down.shape[1] // 4
    chan = lax.axis_index("chan")
    for i in range(4):
        outs[i][...] = down[:, pl.ds(pl.multiple_of((chan ^ i) * width, width), width)]


def combine_kernel(rows, total, got, gain, shift, out):
    half = gain.shape[0]
    means = got[:, 0:half, :]
    mean = jnp.sum(means, axis=0) * (1.0 / got.shape[0])
    var = jnp.sum(got[:, half:, :] + rows * (means - mean) ** 2, axis=0) * (1.0 / total)
    scale = gain[...] / jnp.sqrt(var + 1e-05)
    out[0:half, :] = scale
    out[half:, :] = shift[...] - mean * scale


def hold_kernel(*refs):
    count = (len(refs) - 2) // 2
    sems = refs[-1]
    copies = [pltpu.make_async_copy(refs[i], refs[count + 1 + i], sems.at[i]) for i in range(count)]
    for copy in copies:
        copy.start()
    for copy in copies:
        copy.wait()


def finish_kernel(pieces, bounds, *refs):
    held, refs = refs[: 4 * pieces], refs[4 * pieces :]
    means, scales, weights, out = refs[:4], refs[4:8], refs[8:12], refs[12]
    width = out.shape[1]
    for piece in range(pieces):
        parts = []
        for block in range(4):
            for j in range(width // LANES):
                cut = slice(j * LANES, (j + 1) * LANES)
                a = scales[block][j : j + 1, :] * 0.5
                b = scales[block][width // LANES + j : width // LANES + j + 1, :] * 0.5
                b = b + means[block][piece : piece + 1, cut] * a
                h = held[block * pieces + piece][:, cut].astype(F32) * a + b
                parts.append((h + h * jnp.tanh(h)).astype(BF16))
        swished = jnp.concatenate(parts, axis=1)
        down = jnp.concatenate([w[...] for w in weights], axis=0)
        result = jnp.dot(swished, down, preferred_element_type=F32).astype(BF16)
        at = 0
        for first, size in bounds[piece]:
            out[first : first + size, :] = result[at : at + size]
            at += size


def body(
    features, rec_start, rec_end, w_value, w_gate, depth_kernel, norm_gain, norm_shift, w_down
):
    rows, width = features.shape
    taps_count = depth_kernel.shape[0]
    tms = lax.axis_size("tm")
    total = rows * tms
    chunk = rows // 4
    vmem = pl.BlockSpec(memory_space=pltpu.VMEM)

    first_chunk = features[:chunk]
    rest, _ = lax.optimization_barrier((features, first_chunk))
    linked = [permute(first_chunk, over_link)]
    for k in range(1, 4):
        linked.append(permute(rest[k * chunk : (k + 1) * chunk], over_link))

    weights = pl.pallas_call(
        lay_out_kernel,
        out_shape=[pltpu.VMEM(w_value.shape, BF16)] * 2,
        in_specs=[vmem] * 2,
        out_specs=[vmem] * 2,
        compiler_params=pltpu.CompilerParams(vmem_limit_bytes=8 << 20),
        name="lay_out",
    )(w_value, w_gate)

    halo = jnp.concatenate(
        [
            permute(rest[:8], lambda t, c: (t - 1, c)),
            permute(rest[rows - 8 :], lambda t, c: (t + 1, c)),
        ],
        axis=0,
    )
    halo_linked = permute(halo, over_link)
    halo_mate = permute(halo, to_core)
    halos = [halo, halo_mate, halo_linked, permute(halo_linked, to_core)]

    mate = permute(features, to_core)
    far = []
    for k in range(4):
        far.append(permute(linked[k], to_core))

    taps = jnp.pad(depth_kernel.astype(F32), ((0, 16 - taps_count), (0, 0)))

    downs = pl.pallas_call(
        columns_kernel,
        out_shape=[pltpu.HBM((width, width), BF16)] * 4,
        in_specs=[vmem],
        out_specs=[vmem] * 4,
        compiler_params=pltpu.CompilerParams(vmem_limit_bytes=4 << 20),
        name="columns",
    )(w_down)
    down = [downs[0]]
    for i, move in ((2, over_other_link), (1, to_core), (3, lambda t, c: (t ^ 8, c ^ 3))):
        down.append(permute(downs[i], move))

    edges = [16, chunk - 16, 2 * chunk - 16, 3 * chunk - 16, rows]

    def spread(vector, k):
        part = vector[edges[k] : edges[k + 1]]
        if k == 3:
            part = jnp.concatenate([part, vector[:16]])
        return jnp.broadcast_to(part[:, None], (part.shape[0], LANES))

    starts, ends = [spread(rec_start, k) for k in range(4)], [spread(rec_end, k) for k in range(4)]

    convs, stats, tail, head = [], [], None, None
    for k in range(4):
        if k == 2:
            tail, starts[3], ends[3] = lax.optimization_barrier((tail, starts[3], ends[3]))
        out = stage_call(
            k, taps_count, rows, edges[k], tms, [features, mate, linked[k], far[k]], halos, weights, taps,
            starts[k], ends[k], tail, head, stats,
        )
        convs.append(out[0])
        stats.append(out[1])
        tail = out[2] if k < 3 else None
        head = out[3] if k == 0 else head
    sent = out[2]

    def spread_out(k):
        over = permute(convs[k], over_link)
        mine = permute(convs[k], to_core)
        return convs[k], over, mine, permute(over, to_core)

    pieces = [spread_out(k) for k in range(4)]
    convs = [pieces[k][block] for block in range(4) for k in range(4)]
    means = [stats[3]]
    for move in (over_link, to_core, to_diagonal):
        means.append(permute(stats[3], move))

    got = lax.all_to_all(sent, "tm", 0, 0)
    half = width // LANES
    own_scale = pl.pallas_call(
        functools.partial(combine_kernel, float(rows), float(total)),
        out_shape=pltpu.VMEM((2 * half, LANES), F32),
        in_specs=[vmem] * 3,
        out_specs=vmem,
        compiler_params=pltpu.CompilerParams(vmem_limit_bytes=4 << 20),
        name="combine",
    )(near(got), near(norm_gain.astype(F32).reshape(half, LANES)), near(norm_shift.astype(F32).reshape(half, LANES)))
    scales = [own_scale]
    for move in (over_link, to_core, to_diagonal):
        scales.append(permute(own_scale, move))

    held = [*convs, *down]
    held = pl.pallas_call(
        hold_kernel,
        out_shape=[pltpu.VMEM(c.shape, c.dtype) for c in held],
        in_specs=[pl.BlockSpec(memory_space=pl.ANY)] * len(held) + [vmem],
        out_specs=[vmem] * len(held),
        scratch_shapes=[pltpu.SemaphoreType.DMA((len(held),))],
        compiler_params=pltpu.CompilerParams(vmem_limit_bytes=4 << 20),
        name="hold",
    )(*held, own_scale)
    convs, down = held[: len(convs)], held[len(convs) :]

    bounds = [[(edges[k], edges[k + 1] - edges[k])] for k in range(4)]
    bounds[3].append((0, 16))
    operands = [near(o) for o in [*convs, *means, *scales, *down]]
    return pl.pallas_call(
        functools.partial(finish_kernel, 4, bounds),
        out_shape=jax.ShapeDtypeStruct((rows, width), BF16),
        in_specs=[vmem] * len(operands),
        out_specs=vmem,
        cost_estimate=pl.CostEstimate(
            flops=8 * rows * width * width, transcendentals=rows * 4 * width, bytes_accessed=6 << 20
        ),
        compiler_params=pltpu.CompilerParams(vmem_limit_bytes=16 << 20),
        name="finish",
    )(*operands)


def solution(mesh):
    in_specs = (
        P("tm", "chan"),
        P("tm"),
        P("tm"),
        P(None, "chan"),
        P(None, "chan"),
        P(None, "chan"),
        P("chan"),
        P("chan"),
        P("chan", None),
    )
    out_specs = P("tm", "chan")

    return jax.shard_map(body, mesh=mesh, in_specs=in_specs, out_specs=out_specs, check_vma=False)
```

```python
import functools

import jax
import jax.numpy as jnp
from jax import lax
from jax.experimental import pallas as pl
from jax.experimental.pallas import tpu as pltpu
from jax.sharding import PartitionSpec as P


AXES = ("tm", "chan")
F32, BF16 = jnp.float32, jnp.bfloat16
LANES = 128
TAIL = 32


def permute(value, move):
    tms, chans = lax.axis_size("tm"), lax.axis_size("chan")
    pairs = []
    for t in range(tms):
        for c in range(chans):
            to_t, to_c = move(t, c)
            if 0 <= to_t < tms:
                pairs.append((t * chans + c, to_t * chans + to_c))
    return lax.ppermute(value, AXES, pairs)


def over_link(t, c):
    return t, c ^ 2


def over_other_link(t, c):
    return t ^ 8, c ^ 2


def to_core(t, c):
    return t, c ^ 1


def to_diagonal(t, c):
    return t, c ^ 3


def near(value):
    return pltpu.with_memory_space_constraint(value, pltpu.VMEM)


STEP = 16


def stage_kernel(stage, taps_count, rows, edge, *refs):
    refs = list(refs)
    own, mate, linked, far = [refs.pop(0) for _ in range(4)]
    halos = [refs.pop(0) for _ in range(4)] if stage == 3 else None
    weights = [refs.pop(0) for _ in range(2)]
    taps, start, end = [refs.pop(0) for _ in range(3)]
    tail = refs.pop(0) if stage > 0 else None
    head = refs.pop(0) if stage == 3 else None
    earlier = [refs.pop(0) for _ in range(3)] if stage == 3 else None
    conv_out, stats_out = refs.pop(0), refs.pop(0)
    tail_out = refs.pop(0) if stage < 3 else None
    head_out = refs.pop(0) if stage == 0 else None
    sent_out = refs.pop(0) if stage == 3 else None
    glu, conv = refs

    fresh = linked.shape[0]
    width = weights[0].shape[1]
    blocks = width // LANES
    half = taps_count // 2
    position = lax.axis_index("tm")

    def columns(j):
        return slice(j * LANES, (j + 1) * LANES)

    def put(row, value):
        for j in range(blocks):
            glu[j, row : row + value.shape[0], :] = value[:, columns(j)].astype(F32)

    def gated_of(parts):
        x = jnp.concatenate(parts, axis=1)
        value, gate = [jnp.dot(x, w[...], preferred_element_type=F32) for w in weights]
        return (value * (0.5 + 0.5 * jnp.tanh(0.5 * gate))).astype(BF16)

    if tail is not None:
        put(0, tail[...])
    for row in range(0, fresh, 256):
        at = stage * fresh + row
        parts = [own[at : at + 256, :], mate[at : at + 256, :], linked[row : row + 256, :], far[row : row + 256, :]]
        if halos is not None and row + 256 == fresh:
            parts = [jnp.concatenate([part, halo[...]], axis=0) for part, halo in zip(parts, halos)]
        gated = gated_of(parts)
        put(TAIL + row, gated)
        if head_out is not None and row == 0:
            head_out[...] = gated[:TAIL]
        if tail_out is not None and row + 256 == fresh:
            tail_out[...] = gated[256 - TAIL :]
    if stage == 3:
        put(TAIL + fresh + 16, head[...])

    total_rows = conv_out.shape[0]
    first = TAIL + 16 if stage == 0 else 16
    scale = [[jnp.broadcast_to(taps[k : k + 1, columns(j)], (8, LANES)) for k in range(taps_count)] for j in range(blocks)]
    line = lax.broadcasted_iota(jnp.int32, (STEP, LANES), 0) + position * rows

    def conv_rows(source, target, row, sums):
        frame = line + row
        lo, hi = start[pl.ds(row, STEP), :] - frame, end[pl.ds(row, STEP), :] - frame
        out = []
        for j in range(blocks):
            acc = None
            for k in range(taps_count):
                shift = k - half
                term = glu[j, pl.ds(source + shift, STEP), :]
                term = (term.reshape(STEP // 8, 8, LANES) * scale[j][k][None]).reshape(STEP, LANES)
                if shift < 0:
                    term = jnp.where(lo <= shift, term, 0.0)
                if shift > 0:
                    term = jnp.where(hi > shift, term, 0.0)
                acc = term if acc is None else acc + term
            conv[j, pl.ds(target, STEP), :] = acc
            out.append(sums[j] + jnp.sum(acc.reshape(STEP // 8, 8, LANES), axis=0))
        return tuple(out)

    zero = tuple(jnp.zeros((8, LANES), F32) for _ in range(blocks))
    straight = total_rows - 16 if stage == 3 else total_rows

    def step(i, sums):
        target = pl.multiple_of(i * STEP, STEP)
        return conv_rows(target + first, target, target + edge, sums)

    sums = lax.fori_loop(0, straight // STEP, step, zero, unroll=UNROLL)
    if stage == 3:
        sums = conv_rows(TAIL + fresh + 16, straight, 0, sums)

    means = [jnp.sum(s, axis=0, keepdims=True) * (1.0 / total_rows) for s in sums]
    means8 = [jnp.broadcast_to(m, (8, LANES)) for m in means]

    def centre(i, squares):
        target = pl.multiple_of(i * STEP, STEP)
        out = []
        for j in range(blocks):
            c = conv[j, pl.ds(target, STEP), :].reshape(STEP // 8, 8, LANES) - means8[j][None]
            conv_out[pl.ds(target, STEP), columns(j)] = c.reshape(STEP, LANES).astype(BF16)
            out.append(squares[j] + jnp.sum(c * c, axis=0))
        return tuple(out)

    squares = lax.fori_loop(0, total_rows // STEP, centre, zero, unroll=UNROLL)
    squares = [jnp.sum(q, axis=0, keepdims=True) for q in squares]
    count = jnp.full((1, LANES), float(total_rows), F32)
    if stage < 3:
        for j in range(blocks):
            stats_out[0:1, columns(j)] = means[j]
            stats_out[1:2, columns(j)] = squares[j]
            stats_out[2:3, columns(j)] = count
    else:
        for j in range(blocks):
            for k in range(3):
                stats_out[k : k + 1, columns(j)] = earlier[k][0:1, columns(j)]
            stats_out[3:4, columns(j)] = means[j]
    if sent_out is not None:
        totals = []
        for j in range(blocks):
            parts = [(ref[2:3, columns(j)], ref[0:1, columns(j)], ref[1:2, columns(j)]) for ref in earlier]
            parts.append((count, means[j], squares[j]))
            mean = sum(n * m for n, m, _ in parts) * (1.0 / rows)
            totals.append((mean, sum(q + n * (m - mean) * (m - mean) for n, m, q in parts)))
        piece = jnp.concatenate([t[0] for t in totals] + [t[1] for t in totals], axis=0)
        for i in range(sent_out.shape[0]):
            sent_out[i] = piece


UNROLL = 8


def stage_call(stage, taps_count, rows, edge, count, devices, xs, halos, weights, taps, start, end, tail, head, earlier):
    fresh, width = xs[2].shape[0], weights[0].shape[1]
    margin = pltpu.VMEM((TAIL, width), BF16)
    outs = [pltpu.HBM((count, width), BF16), pltpu.VMEM((8, width), F32)]
    operands = list(xs)
    if stage == 3:
        operands += halos
    operands += [*weights, taps, start, end]
    if stage > 0:
        operands.append(tail)
    if stage == 3:
        operands += [head, *earlier]
    if stage < 3:
        outs.append(margin)
    if stage == 0:
        outs.append(margin)
    if stage == 3:
        outs.append(pltpu.VMEM((devices, 2 * width // LANES, LANES), F32))
    vmem = pl.BlockSpec(memory_space=pltpu.VMEM)
    return pl.pallas_call(
        functools.partial(stage_kernel, stage, taps_count, rows, edge),
        out_shape=outs,
        in_specs=[vmem] * len(operands),
        out_specs=[vmem] * len(outs),
        scratch_shapes=[
            pltpu.VMEM((width // LANES, TAIL + fresh + 16 + TAIL, LANES), F32),
            pltpu.VMEM((width // LANES, count, LANES), F32),
        ],
        cost_estimate=pl.CostEstimate(
            flops=16 * fresh * width * width, transcendentals=fresh * width, bytes_accessed=4 << 20
        ),
        compiler_params=pltpu.CompilerParams(vmem_limit_bytes=12 << 20),
    )(*[near(o) for o in operands])


def lay_out_kernel(value, gate, own_value, own_gate):
    depth = value.shape[0] // 4
    chan = lax.axis_index("chan")
    for i in range(4):
        rows = pl.ds(pl.multiple_of((chan ^ i) * depth, depth), depth)
        own_value[i * depth : (i + 1) * depth, :] = value[rows, :]
        own_gate[i * depth : (i + 1) * depth, :] = gate[rows, :]


def columns_kernel(down, *outs):
    width = down.shape[1] // 4
    chan = lax.axis_index("chan")
    for i in range(4):
        outs[i][...] = down[:, pl.ds(pl.multiple_of((chan ^ i) * width, width), width)]


def combine_kernel(rows, total, pieces, got, gain, shift, centres, out):
    half = gain.shape[0]
    means = got[:, 0:half, :]
    mean = jnp.sum(means, axis=0) * (1.0 / got.shape[0])
    var = jnp.sum(got[:, half:, :] + rows * (means - mean) ** 2, axis=0) * (1.0 / total)
    scale = gain[...] / jnp.sqrt(var + 1e-05)
    out[0:half, :] = scale
    for piece in range(pieces):
        for j in range(half):
            centre = centres[piece : piece + 1, j * LANES : (j + 1) * LANES]
            at = (piece + 1) * half + j
            out[at : at + 1, :] = shift[j : j + 1, :] + (centre - mean[j : j + 1]) * scale[j : j + 1]


def hold_kernel(*refs):
    count = (len(refs) - 2) // 2
    sems = refs[-1]
    copies = [pltpu.make_async_copy(refs[i], refs[count + 1 + i], sems.at[i]) for i in range(count)]
    for copy in copies:
        copy.start()
    for copy in copies:
        copy.wait()


def finish_kernel(pieces, bounds, *refs):
    held, refs = refs[: 4 * pieces], refs[4 * pieces :]
    scales, weights, out = refs[:4], refs[4:8], refs[8]
    width = out.shape[1]
    for piece in range(pieces):
        parts = []
        for block in range(4):
            for j in range(width // LANES):
                cut = slice(j * LANES, (j + 1) * LANES)
                a = scales[block][j : j + 1, :] * 0.5
                at = (piece + 1) * (width // LANES) + j
                b = scales[block][at : at + 1, :] * 0.5
                h = held[block * pieces + piece][:, cut].astype(F32) * a + b
                parts.append((h + h * jnp.tanh(h)).astype(BF16))
        swished = jnp.concatenate(parts, axis=1)
        down = jnp.concatenate([w[...] for w in weights], axis=0)
        result = jnp.dot(swished, down, preferred_element_type=F32).astype(BF16)
        at = 0
        for first, size in bounds[piece]:
            out[first : first + size, :] = result[at : at + size]
            at += size


def body(
    features, rec_start, rec_end, w_value, w_gate, depth_kernel, norm_gain, norm_shift, w_down
):
    rows, width = features.shape
    taps_count = depth_kernel.shape[0]
    tms = lax.axis_size("tm")
    total = rows * tms
    chunk = rows // 4
    vmem = pl.BlockSpec(memory_space=pltpu.VMEM)

    first_chunk = features[:chunk]
    rest, _ = lax.optimization_barrier((features, first_chunk))
    linked = [permute(first_chunk, over_link)]
    for k in range(1, 4):
        linked.append(permute(rest[k * chunk : (k + 1) * chunk], over_link))

    weights = pl.pallas_call(
        lay_out_kernel,
        out_shape=[pltpu.VMEM(w_value.shape, BF16)] * 2,
        in_specs=[vmem] * 2,
        out_specs=[vmem] * 2,
        compiler_params=pltpu.CompilerParams(vmem_limit_bytes=8 << 20),
        name="lay_out",
    )(w_value, w_gate)

    halo = jnp.concatenate(
        [
            permute(rest[:8], lambda t, c: (t - 1, c)),
            permute(rest[rows - 8 :], lambda t, c: (t + 1, c)),
        ],
        axis=0,
    )
    halo_linked = permute(halo, over_link)
    halo_mate = permute(halo, to_core)
    halos = [halo, halo_mate, halo_linked, permute(halo_linked, to_core)]

    mate = permute(features, to_core)
    far = []
    for k in range(4):
        far.append(permute(linked[k], to_core))

    taps = jnp.pad(depth_kernel.astype(F32), ((0, 16 - taps_count), (0, 0)))

    downs = pl.pallas_call(
        columns_kernel,
        out_shape=[pltpu.HBM((width, width), BF16)] * 4,
        in_specs=[vmem],
        out_specs=[vmem] * 4,
        compiler_params=pltpu.CompilerParams(vmem_limit_bytes=4 << 20),
        name="columns",
    )(w_down)
    down = [downs[0]]
    for i, move in ((2, over_other_link), (1, to_core), (3, lambda t, c: (t ^ 8, c ^ 3))):
        down.append(permute(downs[i], move))

    edges = [16, chunk - 16, 2 * chunk - 16, 3 * chunk - 16, rows]

    counts = [edges[k + 1] - edges[k] for k in range(3)] + [rows - edges[3] + 16]
    start = jnp.broadcast_to(rec_start[:, None], (rows, LANES))
    end = jnp.broadcast_to(rec_end[:, None], (rows, LANES))

    convs, stats, tail, head = [], [], None, None
    for k in range(4):
        out = stage_call(
            k, taps_count, rows, edges[k], counts[k], tms, [features, mate, linked[k], far[k]], halos, weights, taps,
            start, end, tail, head, stats,
        )
        convs.append(out[0])
        stats.append(out[1])
        tail = out[2] if k < 3 else None
        head = out[3] if k == 0 else head
    sent = out[2]

    def spread_out(k):
        over = permute(convs[k], over_link)
        mine = permute(convs[k], to_core)
        return convs[k], over, mine, permute(over, to_core)

    pieces = [spread_out(k) for k in range(4)]
    convs = [pieces[k][block] for block in range(4) for k in range(4)]
    got = lax.all_to_all(sent, "tm", 0, 0)
    half = width // LANES
    own_scale = pl.pallas_call(
        functools.partial(combine_kernel, float(rows), float(total), 4),
        out_shape=pltpu.VMEM((16, LANES), F32),
        in_specs=[vmem] * 4,
        out_specs=vmem,
        compiler_params=pltpu.CompilerParams(vmem_limit_bytes=4 << 20),
        name="combine",
    )(
        near(got),
        near(norm_gain.astype(F32).reshape(half, LANES)),
        near(norm_shift.astype(F32).reshape(half, LANES)),
        near(stats[3]),
    )
    scales = [own_scale]
    for move in (over_link, to_core, to_diagonal):
        scales.append(permute(own_scale, move))

    held = [*convs, *down]
    held = pl.pallas_call(
        hold_kernel,
        out_shape=[pltpu.VMEM(c.shape, c.dtype) for c in held],
        in_specs=[pl.BlockSpec(memory_space=pl.ANY)] * len(held) + [vmem],
        out_specs=[vmem] * len(held),
        scratch_shapes=[pltpu.SemaphoreType.DMA((len(held),))],
        compiler_params=pltpu.CompilerParams(vmem_limit_bytes=4 << 20),
        name="hold",
    )(*held, own_scale)
    convs, down = held[: len(convs)], held[len(convs) :]

    bounds = [[(edges[k], edges[k + 1] - edges[k])] for k in range(4)]
    bounds[3].append((0, 16))
    operands = [near(o) for o in [*convs, *scales, *down]]
    return pl.pallas_call(
        functools.partial(finish_kernel, 4, bounds),
        out_shape=jax.ShapeDtypeStruct((rows, width), BF16),
        in_specs=[vmem] * len(operands),
        out_specs=vmem,
        cost_estimate=pl.CostEstimate(
            flops=8 * rows * width * width, transcendentals=rows * 4 * width, bytes_accessed=6 << 20
        ),
        compiler_params=pltpu.CompilerParams(vmem_limit_bytes=16 << 20),
        name="finish",
    )(*operands)


def solution(mesh):
    in_specs = (
        P("tm", "chan"),
        P("tm"),
        P("tm"),
        P(None, "chan"),
        P(None, "chan"),
        P(None, "chan"),
        P("chan"),
        P("chan"),
        P("chan", None),
    )
    out_specs = P("tm", "chan")

    return jax.shard_map(body, mesh=mesh, in_specs=in_specs, out_specs=out_specs, check_vma=False)
```
